32 devices in a mesh: ctx: 4 (over z), head: 4 (over y, x), fsdp: 2 (over core).
Axes of the slice: x: 2, y: 2, z: 4, core: 2. Of those that a mesh axis runs over, the one named last changes fastest.
Arguments:
- query_rows: bfloat16 [4096, 6144], P(('ctx', 'head'), 'fsdp'), may hold values from -400 to 400
- key_rows: bfloat16 [4096, 6144], P(('ctx', 'head'), 'fsdp'), may hold values from -8 to 8
- value_rows: bfloat16 [4096, 4096], P(('ctx', 'head'), 'fsdp'), may hold values from -6 to 6
- query_weight: bfloat16 [1536, 6144], P(('ctx', 'fsdp'), 'head'), may hold values from -6 to 6
- key_weight: bfloat16 [512, 4096], P(('ctx', 'fsdp'), 'head'), may hold values from -6 to 6
Outputs:
- attended: bfloat16 [4096, 4096], P('ctx', ('fsdp', 'head'))
- clipped_query: bfloat16 [1536, 6144], P(('ctx', 'fsdp'), 'head')
- clipped_key: bfloat16 [512, 4096], P(('ctx', 'fsdp'), 'head')
The draws below stay inside these ranges and needn't reach their ends.
All inputs are finite; a program needn't handle non-finite values.
Results may differ from the reference program's by a relative error of at most 0.0033.
Values may be sent and summed in bfloat16 or wider, within the bound.
No kernel may reach another device: no remote copies, remote signals or barrier semaphores. Data moves between devices by JAX's collectives and lax.ppermute only.
A program may use at most 128 MiB of HBM per device.

```python
import math
import jax
import jax.numpy as jnp
from jax import lax

H = 32
DNOPE = 128
DROPE = 64
DV = 128
QR = 1536
KVR = 512
BLK = 1024
DQK = 192
SEQ = 4096


def query_key_pair(key):
    folded = jax.random.fold_in(key, 31)
    subkeys = jax.random.split(folded, 9)
    blocks = SEQ // BLK
    queries = 2.0 * jax.random.normal(subkeys[1], (SEQ, H, DQK), jnp.float32)
    keys_all = jax.random.normal(subkeys[2], (SEQ, H, DQK), jnp.float32)
    hot_slot = BLK // 2 + jax.random.randint(subkeys[3], (blocks, H), 0, BLK // 2)
    key_gap = jax.random.randint(subkeys[4], (blocks, H), 1, BLK // 4 + 1)
    strong = (jax.random.permutation(subkeys[5], H) < H // 2)[None, :]
    order = jax.random.permutation(subkeys[6], blocks)
    top_block = order[jnp.arange(H) % blocks]
    is_top = jnp.arange(blocks)[:, None] == top_block[None, :]
    levels = jax.random.uniform(subkeys[7], (blocks, H), jnp.float32)
    lower_bound = jnp.where(is_top, jnp.where(strong, 220.0, 60.0), jnp.where(strong, 40.0, 30.0))
    upper_bound = jnp.where(is_top, jnp.where(strong, 260.0, 95.0), jnp.where(strong, 140.0, 55.0))
    strength = lower_bound + (upper_bound - lower_bound) * levels
    spread = jax.random.uniform(subkeys[8], (blocks, H), jnp.float32, 1.0, 3.0)
    starts = (jnp.arange(blocks, dtype=jnp.int32) * BLK)[:, None]
    query_at = starts + hot_slot
    key_at = query_at - key_gap
    twin_at = key_at - 1
    head_ids = jnp.broadcast_to(jnp.arange(H, dtype=jnp.int32)[None, :], (blocks, H))
    target = keys_all[key_at, head_ids]
    norm_sq = jnp.sum(target * target, axis=-1, keepdims=True)
    keys_all = keys_all.at[twin_at, head_ids].set(target * (1.0 - spread / strength)[:, :, None])
    queries = queries.at[query_at, head_ids].set(target * (strength * math.sqrt(DQK))[:, :, None] / norm_sq)
    return (queries.reshape(SEQ, H * DQK), keys_all.reshape(SEQ, H * DQK))


def draw_query_rows(key, part):
    return query_key_pair(key)[0].astype(jnp.bfloat16)


def draw_key_rows(key, part):
    return query_key_pair(key)[1].astype(jnp.bfloat16)


def block_scale(key, shape, shards, least, high):
    def one(axis_at, blocks):
        steps = jax.random.uniform(jax.random.fold_in(jax.random.fold_in(key, 6), axis_at), (blocks,), jnp.float32, least / len(shards), high / len(shards))
        return jnp.repeat(jnp.exp(steps), shape[axis_at] // blocks).reshape((-1,) + (1,) * (len(shape) - axis_at - 1))

    level = one(*shards[0])
    for cut in shards[1:]:
        level = level * one(*cut)
    return level


def scatter_about(stream_key, shape, scale, most, cuts=(), kind=jnp.bfloat16):
    result = jax.random.normal(stream_key, shape, jnp.float32) * scale
    if len(cuts) > 0:
        result = block_scale(stream_key, shape, cuts, -0.22, 0.18) * result
    return jnp.clip(result, min=-most, max=most).astype(kind)


def setup_inputs(seed: int = 0) -> dict:
    streams_of = jax.random.split(jax.random.key(seed), 6)
    query_rows = draw_query_rows(jax.random.fold_in(streams_of[5], 71), 0)
    key_rows = draw_key_rows(jax.random.fold_in(streams_of[5], 71), 0)
    value_rows = scatter_about(streams_of[2], (SEQ, H * DV), 1.0, 6.0, ((0, 16), (1, 2)))
    query_weight = scatter_about(streams_of[3], (QR, H * DQK), 1.0, 6.0, ((0, 8), (1, 4)))
    key_weight = scatter_about(streams_of[4], (KVR, H * DNOPE), 1.0, 6.0, ((0, 8), (1, 4)))
    return {"query_rows": query_rows, "key_rows": key_rows, "value_rows": value_rows, "query_weight": query_weight, "key_weight": key_weight}


clip_threshold = 100.0

def partial_softmax(scores, value_block):
    highest = lax.optimization_barrier(jnp.max(scores, axis=2))
    present = jnp.isfinite(highest)
    shifted = jnp.where(present, highest, 0.0)
    weights = jnp.exp(scores - shifted[:, :, None])
    totals = lax.optimization_barrier(jnp.sum(weights, axis=2))
    rounded = lax.optimization_barrier(weights.astype(jnp.bfloat16))
    summed = jnp.einsum('htu,uhd->thd', rounded.astype(jnp.float32), value_block.astype(jnp.float32), precision=lax.Precision.HIGHEST)
    return (summed, totals, jnp.where(present, highest, -jnp.inf))

def merge_parts(own_part, far_part):
    own_sum, own_total, own_high = own_part
    far_sum, far_total, far_high = far_part
    highest = jnp.maximum(own_high, far_high)
    own_scale = jnp.exp(own_high - highest)
    far_scale = jnp.exp(far_high - highest)
    totals = own_total * own_scale + far_total * far_scale
    mixed = own_sum * own_scale.T[:, :, None] + far_sum * far_scale.T[:, :, None]
    return mixed / totals.T[:, :, None]

def take_block(source, first_row, width):
    return lax.dynamic_slice_in_dim(source, first_row, BLK, 0).reshape(BLK, H, width).astype(jnp.float32)

def head_scores(query_cube, key_cube):
    return jnp.einsum('thd,uhd->htu', query_cube, key_cube, precision=lax.Precision.HIGHEST) * DQK ** (-0.5)

def block_attention(block_index, query_rows, key_rows, value_rows):
    first_row = block_index * BLK
    before = jnp.maximum(first_row - BLK, 0)
    query_cube = take_block(query_rows, first_row, DQK)
    key_cube = take_block(key_rows, first_row, DQK)
    value_cube = take_block(value_rows, first_row, DV)
    far_key = take_block(key_rows, before, DQK)
    far_value = take_block(value_rows, before, DV)
    row_ids = lax.broadcasted_iota(jnp.int32, (BLK, BLK), 0)
    col_ids = lax.broadcasted_iota(jnp.int32, (BLK, BLK), 1)
    own_scores = jnp.where((row_ids >= col_ids)[None], head_scores(query_cube, key_cube), -jnp.inf)
    far_scores = jnp.where(block_index > 0, head_scores(query_cube, far_key), -jnp.inf)
    head_peak = jnp.maximum(lax.optimization_barrier(jnp.max(own_scores, axis=(1, 2))), lax.optimization_barrier(jnp.max(far_scores, axis=(1, 2))))
    mixed = merge_parts(partial_softmax(own_scores, value_cube), partial_softmax(far_scores, far_value))
    return (mixed.astype(jnp.bfloat16).reshape(BLK, H * DV), head_peak)

def reference(query_rows, key_rows, value_rows, query_weight, key_weight):
    block_ids = jnp.arange(SEQ // BLK, dtype=jnp.int32)
    attended, peaks = lax.map(lambda index_now: block_attention(index_now, query_rows, key_rows, value_rows), block_ids)
    attended = attended.reshape(SEQ, H * DV)
    head_peak = lax.optimization_barrier(jnp.max(peaks, axis=0))
    factor = jnp.minimum(1.0, clip_threshold / head_peak)
    root_factor = jnp.sqrt(factor)
    column_factor = jnp.concatenate([jnp.broadcast_to(root_factor[:, None], (H, DNOPE)), jnp.broadcast_to(factor[:, None], (H, DROPE))], axis=1)
    clipped_query = (query_weight.astype(jnp.float32).reshape(QR, H, DQK) * column_factor[None]).astype(jnp.bfloat16).reshape(QR, H * DQK)
    clipped_key = (key_weight.astype(jnp.float32).reshape(KVR, H, DNOPE) * root_factor[None, :, None]).astype(jnp.bfloat16).reshape(KVR, H * DNOPE)
    return (attended, clipped_query, clipped_key)
```

```python
import functools
import math

import jax
import jax.numpy as jnp
from jax import lax
from jax.experimental import pallas as pl
from jax.experimental.pallas import tpu as pltpu
from jax.sharding import PartitionSpec as P

DNOPE = 128
DROPE = 64
DV = 128
DQK = 192
PAIR = 2 * DQK
WIDE = 256

clip_threshold = 100.0
SCALE = DQK ** (-0.5)
EXPO = SCALE * math.log2(math.e)


def after(value, *earlier):
    return lax.optimization_barrier((value,) + earlier)[0]


def to_next(value):
    count = lax.axis_size("ctx")
    return lax.ppermute(value, "ctx", [(i, i + 1) for i in range(count - 1)])


def swap(value, axis, step):
    count = lax.axis_size(axis)
    return lax.ppermute(value, axis, [(i, i ^ step) for i in range(count)])


def gather_rows(place, pieces, lanes, dest, place_ref, mask=None):
    rows = pieces[0].shape[0]
    for step, piece in enumerate(pieces):
        if place:
            at = pl.multiple_of((place_ref[0] ^ step) * rows, rows)
        else:
            at = step * rows
        part = piece[:, lanes]
        if mask is not None:
            part = jnp.where(mask, part, jnp.zeros_like(part))
        dest[pl.ds(at, rows), :] = part


def fill(place_ref, causal, queries, keys, query_s, key_s):
    rows = keys[0].shape[0]
    lane = lax.broadcasted_iota(jnp.int32, (rows, WIDE), 1)
    gather_rows(True, queries, slice(0, PAIR), query_s, place_ref)
    for half in range(2):
        lanes = slice(half * 128, half * 128 + WIDE)
        mask = (lane < DQK) if half == 0 else (lane >= WIDE - DQK)
        gather_rows(causal, keys, lanes, key_s.at[half], place_ref, mask)


def own_kernel(count, place_ref, *refs):
    queries, keys = refs[:count], refs[count : 2 * count]
    p_ref, high_ref, total_ref, query_s, key_s = refs[2 * count :]
    tile = pl.program_id(1)
    rows = p_ref.shape[1]
    tiles = query_s.shape[0] // rows

    @pl.when(tile == 0)
    def _():
        fill(place_ref, True, queries, keys, query_s, key_s)

    below = lax.broadcasted_iota(jnp.int32, (rows, rows), 0) >= lax.broadcasted_iota(
        jnp.int32, (rows, rows), 1
    )
    for j in range(tiles):

        @pl.when(tile == j)
        def _(j=j):
            for half in range(2):
                query = query_s[j * rows : (j + 1) * rows, half * 128 : half * 128 + WIDE]
                scores = []
                for u in range(j + 1):
                    s = lax.dot_general(
                        query,
                        key_s[half, u * rows : (u + 1) * rows, :],
                        (((1,), (1,)), ((), ())),
                        preferred_element_type=jnp.float32,
                    )
                    scores.append(jnp.where(below, s, -jnp.inf) if u == j else s)
                high = functools.reduce(jnp.maximum, scores).max(axis=1, keepdims=True)
                total = None
                for u, s in enumerate(scores):
                    p = jnp.exp2((s - high) * EXPO)
                    p_ref[half, :, u * rows : (u + 1) * rows] = p.astype(jnp.bfloat16)
                    total = p if total is None else total + p
                total = total.sum(axis=1, keepdims=True)
                high_ref[half] = jnp.broadcast_to(high, (rows, 128))
                total_ref[half] = jnp.broadcast_to(total, (rows, 128))


def far_kernel(count, place_ref, *refs):
    queries, keys = refs[:count], refs[count : 2 * count]
    (
        high_ref,
        total_ref,
        p_ref,
        own_ref,
        far_ref,
        peak_ref,
        query_s,
        key_s,
    ) = refs[2 * count :]
    tile = pl.program_id(1)
    rows = p_ref.shape[2]
    width = p_ref.shape[3]

    @pl.when(tile == 0)
    def _():
        fill(place_ref, False, queries, keys, query_s, key_s)
        peak_ref[...] = jnp.full(peak_ref.shape, -jnp.inf, jnp.float32)

    at = pl.multiple_of(tile * rows, rows)
    for half in range(2):
        query = query_s[pl.ds(at, rows), half * 128 : half * 128 + WIDE]
        scores = [
            lax.dot_general(
                query,
                key_s[half, u * width : (u + 1) * width, :],
                (((1,), (1,)), ((), ())),
                preferred_element_type=jnp.float32,
            )
            for u in range(count)
        ]
        high = functools.reduce(jnp.maximum, scores).max(axis=1, keepdims=True)
        total = None
        for u, s in enumerate(scores):
            p = jnp.exp2((s - high) * EXPO)
            p_ref[half, u] = p.astype(jnp.bfloat16)
            total = p if total is None else total + p
        total = jnp.broadcast_to(total.sum(axis=1, keepdims=True), (rows, 128))
        high = jnp.broadcast_to(high, (rows, 128))
        high = jnp.where(place_ref[1] > 0, high, -jnp.inf)
        own_high = high_ref[half]
        top = jnp.maximum(own_high, high)
        own_scale = jnp.exp2((own_high - top) * EXPO)
        far_scale = jnp.exp2((high - top) * EXPO)
        share = 1.0 / (own_scale * total_ref[half] + far_scale * total)
        own_ref[half] = own_scale * share
        far_ref[half] = far_scale * share
        peak = jnp.max(top, axis=0, keepdims=True) * SCALE
        peak_ref[half] = jnp.maximum(peak_ref[half], jnp.broadcast_to(peak, (8, 128)))


def mix_kernel(count, place_ref, *refs):
    own_values, far_values = refs[:count], refs[count : 2 * count - 1]
    p_own, p_far, own_ref, far_ref, out_ref, value_s = refs[2 * count - 1 :]
    tile = pl.program_id(1)
    rows = p_own.shape[1]
    tiles = value_s.shape[0] // rows

    @pl.when(tile == 0)
    def _():
        gather_rows(True, own_values, slice(0, 2 * DV), value_s, place_ref)

    for half in range(2):
        lanes = slice(half * DV, (half + 1) * DV)
        far = None
        for u, piece in enumerate(far_values):
            s = jnp.dot(p_far[half, u], piece[:, lanes], preferred_element_type=jnp.float32)
            far = s if far is None else far + s
        far = far * far_ref[half]
        for j in range(tiles):

            @pl.when(tile == j)
            def _(j=j, far=far, half=half, lanes=lanes):
                keys = (j + 1) * rows
                own = jnp.dot(
                    p_own[half, :, :keys], value_s[:keys, lanes], preferred_element_type=jnp.float32
                )
                out_ref[:, lanes] = own * own_ref[half] + far


def last_kernel(value_ref, p_far, far_ref, sum_ref, out_ref):
    for half in range(2):
        lanes = slice(half * DV, (half + 1) * DV)
        far = jnp.dot(p_far[half, 0], value_ref[:, lanes], preferred_element_type=jnp.float32)
        out_ref[:, lanes] = (sum_ref[:, lanes] + far * far_ref[half]).astype(jnp.bfloat16)


def piece_spec(rows, lanes):
    return pl.BlockSpec((rows, lanes), lambda pair, tile, *_: (0, pair))


def own_scores(place, queries, keys):
    count, (rows, lanes) = len(queries), queries[0].shape
    total, heads = count * rows, lanes // DQK
    tile = min(256, total)
    f32 = jnp.float32
    stat = jax.ShapeDtypeStruct((heads, total, 128), f32)
    stat_spec = pl.BlockSpec((2, tile, 128), lambda pair, t, *_: (pair, t, 0))
    return pl.pallas_call(
        functools.partial(own_kernel, count),
        out_shape=(jax.ShapeDtypeStruct((heads, total, total), jnp.bfloat16), stat, stat),
        grid_spec=pltpu.PrefetchScalarGridSpec(
            num_scalar_prefetch=1,
            grid=(heads // 2, total // tile),
            in_specs=[piece_spec(rows, PAIR)] * (2 * count),
            out_specs=(
                pl.BlockSpec((2, tile, total), lambda pair, t, *_: (pair, t, 0)),
                stat_spec,
                stat_spec,
            ),
            scratch_shapes=[
                pltpu.VMEM((total, PAIR), jnp.bfloat16),
                pltpu.VMEM((2, total, WIDE), jnp.bfloat16),
            ],
        ),
        compiler_params=pltpu.CompilerParams(dimension_semantics=("arbitrary", "arbitrary")),
        name="own_scores",
    )(place, *queries, *keys)


def far_scores(place, queries, keys, high, own_total):
    count, (rows, lanes) = len(queries), queries[0].shape
    total, heads = count * rows, lanes // DQK
    tile = min(256, total)
    f32 = jnp.float32
    stat = jax.ShapeDtypeStruct((heads, total, 128), f32)
    stat_spec = pl.BlockSpec((2, tile, 128), lambda pair, t, *_: (pair, t, 0))
    return pl.pallas_call(
        functools.partial(far_kernel, count),
        out_shape=(
            jax.ShapeDtypeStruct((heads, count, total, rows), jnp.bfloat16),
            stat,
            stat,
            jax.ShapeDtypeStruct((heads, 8, 128), f32),
        ),
        grid_spec=pltpu.PrefetchScalarGridSpec(
            num_scalar_prefetch=1,
            grid=(heads // 2, total // tile),
            in_specs=[piece_spec(rows, PAIR)] * (2 * count) + [stat_spec, stat_spec],
            out_specs=(
                pl.BlockSpec((2, count, tile, rows), lambda pair, t, *_: (pair, 0, t, 0)),
                stat_spec,
                stat_spec,
                pl.BlockSpec((2, 8, 128), lambda pair, t, *_: (pair, 0, 0)),
            ),
            scratch_shapes=[
                pltpu.VMEM((total, PAIR), jnp.bfloat16),
                pltpu.VMEM((2, total, WIDE), jnp.bfloat16),
            ],
        ),
        compiler_params=pltpu.CompilerParams(dimension_semantics=("arbitrary", "arbitrary")),
        name="far_scores",
    )(place, *queries, *keys, high, own_total)


def mix(place, own_values, far_values, p_own, p_far, own_share, far_share):
    count, (rows, lanes) = len(own_values), own_values[0].shape
    total, heads = count * rows, lanes // DV
    tile = min(256, total)
    stat_spec = pl.BlockSpec((2, tile, 128), lambda pair, t, *_: (pair, t, 0))
    return pl.pallas_call(
        functools.partial(mix_kernel, count),
        out_shape=jax.ShapeDtypeStruct((total, lanes), jnp.float32),
        grid_spec=pltpu.PrefetchScalarGridSpec(
            num_scalar_prefetch=1,
            grid=(heads // 2, total // tile),
            in_specs=[piece_spec(rows, 2 * DV)] * (2 * count - 1)
            + [
                pl.BlockSpec((2, tile, total), lambda pair, t, *_: (pair, t, 0)),
                pl.BlockSpec((2, count - 1, tile, rows), lambda pair, t, *_: (pair, 0, t, 0)),
                stat_spec,
                stat_spec,
            ],
            out_specs=pl.BlockSpec((tile, 2 * DV), lambda pair, t, *_: (t, pair)),
            scratch_shapes=[pltpu.VMEM((total, 2 * DV), jnp.bfloat16)],
        ),
        compiler_params=pltpu.CompilerParams(dimension_semantics=("arbitrary", "arbitrary")),
        name="mix",
    )(place, *own_values, *far_values, p_own, p_far, own_share, far_share)


def last(value, p_far, far_share, partial):
    rows, lanes = value.shape
    total, heads = partial.shape[0], lanes // DV
    count = p_far.shape[1]
    tile = min(512, total)
    return pl.pallas_call(
        last_kernel,
        out_shape=jax.ShapeDtypeStruct((total, lanes), jnp.bfloat16),
        grid=(heads // 2, total // tile),
        in_specs=[
            pl.BlockSpec((rows, 2 * DV), lambda pair, t: (0, pair)),
            pl.BlockSpec((2, 1, tile, rows), lambda pair, t: (pair, count - 1, t, 0)),
            pl.BlockSpec((2, tile, 128), lambda pair, t: (pair, t, 0)),
            pl.BlockSpec((tile, 2 * DV), lambda pair, t: (t, pair)),
        ],
        out_specs=pl.BlockSpec((tile, 2 * DV), lambda pair, t: (t, pair)),
        compiler_params=pltpu.CompilerParams(dimension_semantics=("arbitrary", "arbitrary")),
        name="last",
    )(value, p_far, far_share, partial)


def shared_peak(peak, axis):
    count = lax.axis_size(axis)
    if count <= 4:
        parts = [peak] + [swap(peak, axis, step) for step in range(1, count)]
        return functools.reduce(jnp.maximum, parts)
    step = 1
    while step < count:
        peak = jnp.maximum(peak, swap(peak, axis, step))
        step *= 2
    return peak


def wanted_peaks(peak, weight_heads):
    heads = lax.axis_size("head")
    cores = lax.axis_size("fsdp")
    each = peak.shape[0]
    wide = weight_heads // each
    found = []
    for turn in range(wide):
        pairs = []
        for head in range(heads):
            for core in range(cores):
                group = head * wide + (core + turn) % wide
                source = (group % heads) * cores + group // heads
                pairs.append((source, head * cores + core))
        found.append(lax.ppermute(peak, ("head", "fsdp"), pairs))
    core = lax.axis_index("fsdp")
    ordered = []
    for slot in range(wide):
        value = found[0]
        for turn in range(1, wide):
            value = jnp.where((core + turn) % wide == slot, found[turn], value)
        ordered.append(value)
    return jnp.concatenate(ordered)


def body(query_rows, key_rows, value_rows, query_weight, key_weight):
    heads_at = lax.axis_index("head")
    count = lax.axis_size("head")

    def block(source, step):
        width = source.shape[1] // count
        return lax.dynamic_slice_in_dim(source, (heads_at ^ step) * width, width, 1)

    steps = range(1, count)
    key = [block(key_rows, 0)]
    far_key = [to_next(key[0])]
    key += [swap(block(key_rows, s), "head", s) for s in steps]
    value = [block(value_rows, 0)]
    far_value = [to_next(value[0])]
    query = [block(query_rows, 0)] + [swap(block(query_rows, s), "head", s) for s in steps]
    value += [swap(block(value_rows, s), "head", s) for s in steps]
    far_key += [to_next(k) for k in key[1:]]
    far_value += [to_next(v) for v in value[1:]]

    block_index = lax.axis_index("ctx")
    place = jnp.stack([heads_at, block_index]).astype(jnp.int32)
    p_own, own_high, own_total = own_scores(place, query, key)
    p_far, own_share, far_share, peaks = far_scores(place, query, far_key, own_high, own_total)
    local_peak = shared_peak(peaks[:, 0, 0], "ctx")
    partial = mix(place, value, far_value[:-1], p_own, p_far, own_share, far_share)
    attended = last(far_value[-1], p_far, far_share, partial)

    weight_heads = key_weight.shape[1] // DNOPE
    own_peaks = wanted_peaks(local_peak, weight_heads)
    factor = jnp.minimum(1.0, clip_threshold / own_peaks)
    root_factor = jnp.sqrt(factor)
    column_factor = jnp.concatenate(
        [
            jnp.broadcast_to(root_factor[:, None], (weight_heads, DNOPE)),
            jnp.broadcast_to(factor[:, None], (weight_heads, DROPE)),
        ],
        axis=1,
    ).reshape(1, weight_heads * DQK)
    key_factor = jnp.broadcast_to(root_factor[:, None], (weight_heads, DNOPE)).reshape(1, -1)
    clipped_query = (query_weight.astype(jnp.float32) * column_factor).astype(jnp.bfloat16)
    clipped_key = (key_weight.astype(jnp.float32) * key_factor).astype(jnp.bfloat16)
    return (attended, clipped_query, clipped_key)


def solution(mesh):
    return jax.shard_map(
        body,
        mesh=mesh,
        in_specs=(
            P(("ctx", "head"), "fsdp"),
            P(("ctx", "head"), "fsdp"),
            P(("ctx", "head"), "fsdp"),
            P(("ctx", "fsdp"), "head"),
            P(("ctx", "fsdp"), "head"),
        ),
        out_specs=(
            P("ctx", ("fsdp", "head")),
            P(("ctx", "fsdp"), "head"),
            P(("ctx", "fsdp"), "head"),
        ),
        check_vma=False,
    )
```

```python
import functools
import math

import jax
import jax.numpy as jnp
from jax import lax
from jax.experimental import pallas as pl
from jax.experimental.pallas import tpu as pltpu
from jax.sharding import PartitionSpec as P


DNOPE = 128
DROPE = 64
DV = 128
DQK = 192
PAIR = 2 * DQK
WIDE = 256

clip_threshold = 100.0
SCALE = DQK ** (-0.5)
EXPO = SCALE * math.log2(math.e)


def after(value, *earlier):
    return lax.optimization_barrier((value,) + earlier)[0]


def to_next(value, ring=True):
    count = lax.axis_size("ctx")
    pairs = [(i, (i + 1) % count) for i in range(count if ring else count - 1)]
    return lax.ppermute(value, "ctx", pairs)


def swap(value, axis, step):
    count = lax.axis_size(axis)
    return lax.ppermute(value, axis, [(i, i ^ step) for i in range(count)])


def row_span(place_ref, step, rows):
    return pl.ds(pl.multiple_of((place_ref[0] ^ step) * rows, rows), rows)


def head_lanes(head):
    start = (head // 2) * PAIR + (head % 2) * (PAIR - WIDE)
    return slice(start, start + WIDE)


def keep_keys(piece, head):
    part = piece[:, head_lanes(head)]
    lane = lax.broadcasted_iota(jnp.int32, part.shape, 1)
    mask = (lane < DQK) if head % 2 == 0 else (lane >= WIDE - DQK)
    return jnp.where(mask, part, jnp.zeros_like(part))


def dot_keys(query, key):
    return lax.dot_general(
        query, key, (((1,), (1,)), ((), ())), preferred_element_type=jnp.float32
    )


def softmax_parts(scores, store):
    high = functools.reduce(jnp.maximum, scores).max(axis=1, keepdims=True)
    total = None
    for u, s in enumerate(scores):
        p = jnp.exp2((s - high) * EXPO)
        store(u, p.astype(jnp.bfloat16))
        total = p if total is None else total + p
    return high, total.sum(axis=1, keepdims=True)


def by_lane(columns):
    shape = (columns[0].shape[0], 128)
    lane = lax.broadcasted_iota(jnp.int32, shape, 1)
    packed = jnp.broadcast_to(columns[0], shape)
    for head in range(1, len(columns)):
        packed = jnp.where(lane == head, columns[head], packed)
    return packed


def from_lane(packed, head):
    return jnp.broadcast_to(packed[:, head : head + 1], (packed.shape[0], 128))


def cut_kernel(steps, place_ref, source_ref, *refs):
    pieces, sems = refs[:-1], refs[-1]
    width = pieces[0].shape[1]
    copies = []
    for at, (step, piece) in enumerate(zip(steps, pieces)):
        start = pl.multiple_of((place_ref[0] ^ step) * width, 128)
        copies.append(
            pltpu.make_async_copy(source_ref.at[:, pl.ds(start, width)], piece, sems.at[at])
        )
    for copy in copies:
        copy.start()
    for copy in copies:
        copy.wait()


def own_kernel(steps, fresh, place_ref, *refs):
    parts = len(steps)
    queries = refs[:parts]
    p_ref, high_ref, total_ref, key_ref, query_s = refs[-5:]
    heads, size, _ = p_ref.shape
    rows = queries[0].shape[0]
    count = size // rows
    if fresh:
        for step, piece in enumerate(refs[parts:-5]):
            for head in range(heads):
                key_ref[head, row_span(place_ref, step, rows), :] = keep_keys(piece, head)
    else:
        key_ref = refs[parts]
    for part in range(parts):
        query_s[part] = queries[part][...]
    below = lax.broadcasted_iota(jnp.int32, (rows, rows), 0) >= lax.broadcasted_iota(
        jnp.int32, (rows, rows), 1
    )

    def piece_step(part, carry):
        step = steps[0]
        for at in range(1, parts):
            step = jnp.where(part == at, steps[at], step)
        position = place_ref[0] ^ step
        for j in range(count):

            @pl.when(position == j)
            def _(j=j):
                span = slice(j * rows, (j + 1) * rows)
                highs, totals = [], []
                for head in range(heads):
                    query = query_s[part, :, head_lanes(head)]
                    scores = []
                    for u in range(j + 1):
                        s = dot_keys(query, key_ref[head, u * rows : (u + 1) * rows, :])
                        scores.append(jnp.where(below, s, -jnp.inf) if u == j else s)

                    def store(u, p, head=head):
                        p_ref[head, span, u * rows : (u + 1) * rows] = p

                    high, total = softmax_parts(scores, store)
                    highs.append(high)
                    totals.append(total)
                high_ref[span] = by_lane(highs)
                total_ref[span] = by_lane(totals)

        return carry

    lax.fori_loop(0, parts, piece_step, 0)


def far_kernel(steps, fresh, place_ref, *refs):
    parts = len(steps)
    queries = refs[:parts]
    p_ref, high_ref, total_ref, key_ref = refs[-4:]
    heads, _, width = p_ref.shape
    rows = queries[0].shape[0]
    if fresh:
        for at, piece in enumerate(refs[parts:-4]):
            for head in range(heads):
                key_ref[head, at * rows : (at + 1) * rows, :] = keep_keys(piece, head)
    else:
        key_ref = refs[parts]
    for step, piece in zip(steps, queries):
        span = row_span(place_ref, step, rows)
        highs, totals = [], []
        for head in range(heads):
            query = piece[:, head_lanes(head)]
            scores = [
                dot_keys(query, key_ref[head, u * rows : (u + 1) * rows, :])
                for u in range(width // rows)
            ]

            def store(u, p, head=head, span=span):
                p_ref[head, span, u * rows : (u + 1) * rows] = p

            high, total = softmax_parts(scores, store)
            highs.append(high)
            totals.append(total)
        high_ref[span] = by_lane(highs)
        total_ref[span] = by_lane(totals)


def merge_kernel(count, place_ref, *refs):
    queries, key = refs[:count], refs[count]
    own_high, own_total, far_high, far_total = refs[count + 1 : count + 5]
    p_ref, own_ref, far_ref, end_ref, peak_ref = refs[count + 5 :]
    heads, _, rows = p_ref.shape
    near = place_ref[1] > 0
    keys = [keep_keys(key, head) for head in range(heads)]
    peak = None
    for step, piece in enumerate(queries):
        span = row_span(place_ref, step, rows)
        highs, totals = [], []
        for head in range(heads):

            def store(u, p, head=head, span=span):
                p_ref[head, span] = p

            high, total = softmax_parts([dot_keys(piece[:, head_lanes(head)], keys[head])], store)
            highs.append(high)
            totals.append(total)
        end_high = jnp.where(near, by_lane(highs), -jnp.inf)
        far = jnp.where(near, far_high[span], -jnp.inf)
        own = own_high[span]
        top = jnp.maximum(own, jnp.maximum(far, end_high))
        own_scale = jnp.exp2((own - top) * EXPO)
        far_scale = jnp.exp2((far - top) * EXPO)
        end_scale = jnp.exp2((end_high - top) * EXPO)
        share = 1.0 / (
            own_scale * own_total[span] + far_scale * far_total[span] + end_scale * by_lane(totals)
        )
        own_ref[span] = own_scale * share
        far_ref[span] = far_scale * share
        end_ref[span] = end_scale * share
        best = jnp.max(top, axis=0, keepdims=True)
        peak = best if peak is None else jnp.maximum(peak, best)
    peak_ref[...] = jnp.broadcast_to(peak * SCALE, peak_ref.shape)


def mix_kernel(count, place_ref, *refs):
    own_values, far_values = refs[:count], refs[count : 2 * count - 1]
    p_own, p_far, own_ref, far_ref, out_ref, value_s = refs[2 * count - 1 :]
    rows = own_values[0].shape[0]
    for step, piece in enumerate(own_values):
        value_s[row_span(place_ref, step, rows), :] = piece[...]
    for head in range(p_own.shape[0]):
        lanes = slice(head * DV, (head + 1) * DV)
        for j in range(count):
            span = slice(j * rows, (j + 1) * rows)
            far = None
            for u, piece in enumerate(far_values):
                s = jnp.dot(
                    p_far[head, span, u * rows : (u + 1) * rows],
                    piece[:, lanes],
                    preferred_element_type=jnp.float32,
                )
                far = s if far is None else far + s
            keys = (j + 1) * rows
            own = jnp.dot(
                p_own[head, span, :keys], value_s[:keys, lanes], preferred_element_type=jnp.float32
            )
            out_ref[span, lanes] = own * from_lane(own_ref[span], head) + far * from_lane(
                far_ref[span], head
            )


def last_kernel(value_ref, p_ref, end_ref, sum_ref, out_ref):
    heads, size, rows = p_ref.shape
    for head in range(heads):
        lanes = slice(head * DV, (head + 1) * DV)
        for j in range(size // rows):
            span = slice(j * rows, (j + 1) * rows)
            far = jnp.dot(p_ref[head, span], value_ref[:, lanes], preferred_element_type=jnp.float32)
            out_ref[span, lanes] = (
                sum_ref[span, lanes] + far * from_lane(end_ref[span], head)
            ).astype(jnp.bfloat16)


def local_call(kernel, out_shape, place, operands, scratch=(), aliases=None, far=False):
    near = pl.BlockSpec(memory_space=pltpu.VMEM)
    specs = [pl.BlockSpec(memory_space=pltpu.HBM) if far else near] * len(operands)
    if place is not None:
        specs, operands = [pl.BlockSpec(memory_space=pltpu.SMEM)] + specs, [place] + operands
    return pl.pallas_call(
        kernel,
        out_shape=out_shape,
        in_specs=specs,
        out_specs=jax.tree.map(lambda _: near, out_shape),
        scratch_shapes=scratch,
        input_output_aliases=aliases or {},
        compiler_params=pltpu.CompilerParams(vmem_limit_bytes=8 << 20),
    )(*operands)


def cut(place, source, steps, count):
    shape = jax.ShapeDtypeStruct((source.shape[0], source.shape[1] // count), source.dtype)
    return local_call(
        functools.partial(cut_kernel, tuple(steps)),
        (shape,) * len(steps),
        place,
        [source],
        [pltpu.SemaphoreType.DMA((len(steps),))],
        far=True,
    )


def scores(kernel, place, steps, queries, keys, width, earlier, scratch):
    (rows, lanes), heads = queries[0].shape, queries[0].shape[1] // DQK
    total = lax.axis_size("head") * rows
    stat = jax.ShapeDtypeStruct((total, 128), jnp.float32)
    shapes = (jax.ShapeDtypeStruct((heads, total, width), jnp.bfloat16), stat, stat)
    prepared = jax.ShapeDtypeStruct((heads, width, WIDE), jnp.bfloat16)
    body = functools.partial(kernel, tuple(steps), earlier is None)
    if earlier is None:
        return local_call(body, shapes + (prepared,), place, [*queries, *keys], scratch)
    p, high, sums, ready = earlier
    first = len(queries) + 2
    aliases = {first: 0, first + 1: 1, first + 2: 2}
    operands = [*queries, ready, p, high, sums]

    def aliased(*refs):
        body(*refs[: first], *refs[first + 3 : first + 6], None, *refs[first + 6 :])

    return local_call(aliased, shapes, place, operands, scratch, aliases)


def own_scores(place, steps, queries, keys, earlier=None):
    rows, lanes = queries[0].shape
    width = rows * lax.axis_size("head")
    scratch = [pltpu.VMEM((len(steps), rows, lanes), jnp.bfloat16)]
    return scores(own_kernel, place, steps, queries, keys, width, earlier, scratch)


def far_scores(place, steps, queries, keys, earlier=None):
    width = queries[0].shape[0] * (lax.axis_size("head") - 1)
    return scores(far_kernel, place, steps, queries, keys, width, earlier, [])


def merge(place, queries, key, stats):
    count, (rows, lanes) = len(queries), key.shape
    stat = jax.ShapeDtypeStruct((count * rows, 128), jnp.float32)
    return local_call(
        functools.partial(merge_kernel, count),
        (
            jax.ShapeDtypeStruct((lanes // DQK, count * rows, rows), jnp.bfloat16),
            stat,
            stat,
            stat,
            jax.ShapeDtypeStruct((8, 128), jnp.float32),
        ),
        place,
        [*queries, key, *stats],
    )


def mix(place, own_values, far_values, parts):
    count, (rows, lanes) = len(own_values), own_values[0].shape
    return local_call(
        functools.partial(mix_kernel, count),
        jax.ShapeDtypeStruct((count * rows, lanes), jnp.float32),
        place,
        [*own_values, *far_values, *parts],
        [pltpu.VMEM((count * rows, lanes), jnp.bfloat16)],
    )


def last(value, p_end, end_share, partial):
    return local_call(
        last_kernel,
        jax.ShapeDtypeStruct(partial.shape, jnp.bfloat16),
        None,
        [value, p_end, end_share, partial],
    )


def top_kernel(*refs):
    refs[-1][...] = functools.reduce(jnp.maximum, [ref[...] for ref in refs[:-1]])


def top_of(parts):
    shape = jax.ShapeDtypeStruct(parts[0].shape, parts[0].dtype)
    return local_call(top_kernel, shape, None, list(parts))


def shared_peak(peak, axis):
    count = lax.axis_size(axis)
    if count <= 4:
        return top_of([peak] + [swap(peak, axis, step) for step in range(1, count)])
    step = 1
    while step < count:
        peak = top_of([peak, swap(peak, axis, step)])
        step *= 2
    return peak


def wanted_peaks(peak, wide):
    heads = lax.axis_size("head")
    cores = lax.axis_size("fsdp")
    found = []
    for turn in range(wide):
        pairs = []
        for head in range(heads):
            for core in range(cores):
                group = head * wide + (core + turn) % wide
                source = (group % heads) * cores + group // heads
                pairs.append((source, head * cores + core))
        found.append(lax.ppermute(peak, ("head", "fsdp"), pairs))
    return found


def clip_kernel(wide, place_ref, *refs):
    found, (query_ref, key_ref, query_out, key_out) = refs[:wide], refs[wide:]
    each = key_ref.shape[1] // DNOPE // wide
    lane = lax.broadcasted_iota(jnp.int32, (1, 128), 1)
    for slot in range(wide):
        peaks = found[0][:1, :]
        for turn in range(1, wide):
            peaks = jnp.where((place_ref[2] + turn) % wide == slot, found[turn][:1, :], peaks)
        factor = jnp.minimum(1.0, clip_threshold / peaks)
        root = jnp.sqrt(factor)
        for even in range(0, each, 2):
            full = [from_lane(factor, head) for head in (even, even + 1)]
            half = [from_lane(root, head) for head in (even, even + 1)]
            start = (slot * each + even) * DQK
            lanes_of = {
                start: half[0],
                start + 128: jnp.where(lane < DROPE, full[0], half[1]),
                start + 256: jnp.where(lane < DROPE, half[1], full[1]),
            }
            for at, row in lanes_of.items():
                part = query_ref[:, at : at + 128].astype(jnp.float32) * row
                query_out[:, at : at + 128] = part.astype(jnp.bfloat16)
            for odd in range(2):
                at = (slot * each + even + odd) * DNOPE
                part = key_ref[:, at : at + DNOPE].astype(jnp.float32) * half[odd]
                key_out[:, at : at + DNOPE] = part.astype(jnp.bfloat16)


def clip(place, found, query_weight, key_weight):
    return local_call(
        functools.partial(clip_kernel, len(found)),
        tuple(jax.ShapeDtypeStruct(w.shape, w.dtype) for w in (query_weight, key_weight)),
        place,
        [*found, query_weight, key_weight],
    )


def program(query_rows, key_rows, value_rows, query_weight, key_weight):
    count = lax.axis_size("head")
    steps = list(range(count))
    end = count - 1
    place = jnp.stack([lax.axis_index(name) for name in ("head", "ctx", "fsdp")]).astype(jnp.int32)

    def spread(pieces):
        return pieces[:1] + [swap(pieces[s], "head", s) for s in steps[1:]]

    def onward(pieces):
        return [to_next(pieces[s], s < end) for s in steps]

    key = spread(list(cut(place, key_rows, steps, count)))
    value = spread(list(cut(place, value_rows, steps, count)))
    query = spread(list(cut(place, query_rows, steps, count)))
    far_key, far_value = onward(key), onward(value)

    first, second = steps[: count // 2], steps[count // 2 :]
    *own, own_keys = own_scores(place, first, [query[s] for s in first], key)
    *far, far_keys = far_scores(place, first, [query[s] for s in first], far_key[:end])
    own = own_scores(place, second, [query[s] for s in second], None, (*own, own_keys))
    far = far_scores(place, second, [query[s] for s in second], None, (*far, far_keys))
    p_end, own_share, far_share, end_share, peaks = merge(
        place, query, far_key[end], [*own[1:], *far[1:]]
    )
    partial = mix(place, value, far_value[:end], [own[0], far[0], own_share, far_share])
    found = wanted_peaks(shared_peak(peaks, "ctx"), lax.axis_size("fsdp"))
    clipped_query, clipped_key = clip(place, found, query_weight, key_weight)
    partial = after(partial, clipped_query, clipped_key)
    attended = last(far_value[end], p_end, end_share, partial)
    return (attended, clipped_query, clipped_key)


def solution(mesh):
    return sharded(mesh)


def sharded(mesh):
    return jax.shard_map(
        program,
        mesh=mesh,
        in_specs=(
            P(("ctx", "head"), "fsdp"),
            P(("ctx", "head"), "fsdp"),
            P(("ctx", "head"), "fsdp"),
            P(("ctx", "fsdp"), "head"),
            P(("ctx", "fsdp"), "head"),
        ),
        out_specs=(
            P("ctx", ("fsdp", "head")),
            P(("ctx", "fsdp"), "head"),
            P(("ctx", "fsdp"), "head"),
        ),
        check_vma=False,
    )
```
